512 devices in a mesh: dp: 32 (over y, x), expert: 16 (over z, core).
Axes of the slice: x: 4, y: 8, z: 8, core: 2. Of those that a mesh axis runs over, the one named last changes fastest.
Arguments:
- features: bfloat16 [16384, 1536], P(('dp', 'expert')), may hold values from -6 to 6
- classes: int32 [16384], P(('dp', 'expert')), may hold values from 0 to 15, as said below
- live_counts: int32 [512], P(('dp', 'expert')), may hold values from 2 to 32, as said below
- cotangent: bfloat16 [16384, 1536], P(('dp', 'expert')), may hold values from -0.75 to 0.75
- up_weight: bfloat16 [16, 6144, 1536], P('expert', 'dp'), may hold values from -0.15625 to 0.15625
- down_weight: bfloat16 [16, 6144, 1536], P('expert', 'dp'), may hold values from -0.078125 to 0.078125
Outputs:
- mixed: bfloat16 [16384, 1536], P(('dp', 'expert'))
- up_grad: float32 [16, 6144, 1536], P('expert', 'dp')
- down_grad: float32 [16, 6144, 1536], P('expert', 'dp')
The draws below stay inside these ranges and needn't reach their ends.
Inputs may be any that keep to these rules, and one draw needn't show every extreme that they name: `classes`: each device's 32 slots name every class exactly 2 times, and slots 0 to 1 of every device name one common class. `live_counts`: entry i counts the live slots of device i, which are its first ones; some device has all 32 live.
All inputs are finite; a program needn't handle non-finite values.
Results may differ from the reference program's by a relative error of at most 0.02.
Values may be sent and summed in bfloat16 or wider, within the bound.
A program may use at most 64 MiB of HBM per device.

```python
from functools import partial
import jax
import jax.numpy as jnp
from jax import lax

D = 1536
FF = 6144
EXPERTS = 16
ROWS = 32
CAP = 2
TOKENS = 16384
N_DP = 32
DEVICES = 512


def draw_classes(key, part):
    hot_class = jax.random.randint(jax.random.fold_in(key, 11), (), 0, EXPERTS)
    ordered = jnp.arange(ROWS, dtype=jnp.int32) // CAP
    others = ordered[CAP:]
    device_keys = jax.random.split(jax.random.fold_in(key, 12), DEVICES)
    shuffled = jax.vmap(lambda sub_key: jax.random.permutation(sub_key, others))(device_keys)
    leading = jnp.zeros((DEVICES, CAP), jnp.int32)
    table = jnp.concatenate([leading, shuffled], axis=1)
    return ((table + hot_class) % EXPERTS).reshape(-1).astype(jnp.int32)


def draw_live_counts(key, part):
    counts = jax.random.randint(jax.random.fold_in(key, 21), (DEVICES,), CAP, ROWS + 1)
    full_device = jax.random.randint(jax.random.fold_in(key, 22), (), 0, DEVICES)
    index = jnp.arange(DEVICES, dtype=jnp.int32)
    return jnp.where(index == full_device, ROWS, counts).astype(jnp.int32)


def steps_of(stream_key, shape, cuts, smallest, high):
    loudness = 1.0
    for dim, blocks in cuts:
        draws = jax.random.uniform(jax.random.fold_in(jax.random.fold_in(stream_key, 6), dim), (blocks,), jnp.float32, smallest / len(cuts), high / len(cuts))
        loudness = loudness * jnp.repeat(jnp.exp(draws), shape[dim] // blocks).reshape((-1,) + (1,) * (len(shape) - 1 - dim))
    return loudness


def centred(key, dims, width, most, cuts=(), kind=jnp.bfloat16):
    gain = steps_of(key, dims, cuts, -0.22, 0.18) if cuts else 1.0
    drawn = jax.random.normal(key, dims, jnp.float32) * width * gain
    return jnp.minimum(jnp.maximum(drawn, -most), most).astype(kind)


def setup_inputs(seed: int = 0) -> dict:
    seeds = jax.random.split(jax.random.key(seed), 7)
    features = centred(seeds[0], (TOKENS, D), 1.0, 6.0, ((0, 512),))
    classes = draw_classes(jax.random.fold_in(seeds[6], 71), 0)
    live_counts = draw_live_counts(jax.random.fold_in(seeds[6], 71), 0)
    cotangent = centred(seeds[3], (TOKENS, D), 0.125, 0.75, ((0, 512),))
    up_weight = centred(seeds[4], (EXPERTS, FF, D), D ** -0.5, 0.15625, ((0, 16), (1, 32)))
    down_weight = centred(seeds[5], (EXPERTS, FF, D), FF ** -0.5, 0.078125, ((0, 16), (1, 32)))
    return dict(features=features, classes=classes, live_counts=live_counts, cotangent=cotangent, up_weight=up_weight, down_weight=down_weight)


def expert_pass(item):
    rows, grads, up_rows, down_rows = item
    inner = jnp.dot(rows, up_rows.T, preferred_element_type=jnp.float32)
    hidden = jax.nn.gelu(inner, approximate=True).astype(jnp.bfloat16)
    slope = jnp.dot(grads, down_rows.T, preferred_element_type=jnp.float32)
    _, pull = jax.vjp(partial(jax.nn.gelu, approximate=True), inner)
    inner_grad = pull(slope)[0].astype(jnp.bfloat16)
    grad_up = jnp.dot(inner_grad.T, rows, preferred_element_type=jnp.float32)
    grad_down = jnp.dot(hidden.T, grads, preferred_element_type=jnp.float32)
    slice_width = FF // N_DP
    hidden_parts = hidden.reshape(hidden.shape[0], N_DP, slice_width).transpose(1, 0, 2)
    down_parts = down_rows.reshape(N_DP, slice_width, D)

    def add_part(total, pair):
        term = jnp.dot(pair[0], pair[1], preferred_element_type=jnp.float32)
        rounded = lax.optimization_barrier(term.astype(jnp.bfloat16))
        return (total + rounded.astype(jnp.float32), None)
    start_total = jnp.zeros((hidden.shape[0], D), jnp.float32)
    total, _ = lax.scan(add_part, start_total, (hidden_parts, down_parts))
    return (total.astype(jnp.bfloat16), grad_up, grad_down)

def reference(features, classes, live_counts, cotangent, up_weight, down_weight):
    position = jnp.arange(TOKENS, dtype=jnp.int32) % ROWS
    limit = jnp.repeat(live_counts, ROWS)
    keep = (position < limit).astype(features.dtype)[:, None]
    order = jnp.argsort(classes, stable=True).astype(jnp.int32)
    sorted_rows = (features * keep)[order].reshape(EXPERTS, DEVICES * CAP, D)
    sorted_grads = (cotangent * keep)[order].reshape(EXPERTS, DEVICES * CAP, D)
    outputs, grad_up, grad_down = lax.map(expert_pass, (sorted_rows, sorted_grads, up_weight, down_weight))
    mixed = jnp.zeros((TOKENS, D), outputs.dtype).at[order].set(outputs.reshape(TOKENS, D))
    return (mixed, grad_up, grad_down)
```

```python
import functools

import jax
import jax.numpy as jnp
from jax import lax
from jax.experimental import pallas as pl
from jax.experimental.pallas import tpu as pltpu
from jax.sharding import PartitionSpec as P

NY, NX = 8, 4
MESH = pl.DeviceIdType.MESH
SEMS = 52
ROOT = 0.7978845608028654
CUBE = 0.044715


def slot_table(group_classes, group_counts, span, expert_count):
    row_count = group_classes.shape[0]
    position = lax.broadcasted_iota(jnp.int32, (1, row_count), 1)
    live = position < group_counts
    same = group_classes[:, None] == group_classes[None, :]
    later = lax.broadcasted_iota(jnp.int32, (row_count, row_count), 0)
    sooner = lax.broadcasted_iota(jnp.int32, (row_count, row_count), 1)
    place = jnp.sum((same & (sooner < later)).astype(jnp.int32), axis=1)
    target = group_classes * span + place
    slots = lax.broadcasted_iota(jnp.int32, (expert_count * span, 1), 0)
    chosen = (target[None, :] == slots) & live
    return chosen.astype(jnp.bfloat16)


class Line:
    def __init__(self, count, here, view, right, left, sems, take, sent):
        self.count, self.here, self.view = count, here, view
        self.right, self.left = right, left
        self.send_sem, self.recv_sem = sems
        self.base = take(count)
        self.sent = sent

    def at(self, offset):
        return lax.rem(self.here + offset + self.count, self.count)

    def rows(self, half, way):
        rows = 32
        if not half:
            return pl.ds(0, rows)
        return pl.ds(0, rows // 2) if way == 0 else pl.ds(rows // 2, rows // 2)

    def copy(self, step, way, src, dst):
        k = self.base + 2 * (step - 1) + way
        return pltpu.make_async_remote_copy(
            src_ref=src,
            dst_ref=dst,
            send_sem=self.send_sem.at[k],
            recv_sem=self.recv_sem.at[k],
            device_id=self.right if way == 0 else self.left,
            device_id_type=MESH,
        )


class Spread(Line):
    def start(self, step):
        for way, sign in ((0, -1), (1, 1)):
            ref = self.view(self.at(sign * (step - 1)), self.rows(step == self.count // 2, way))
            copy = self.copy(step, way, ref, ref)
            copy.start()
            self.sent.append(copy)

    def wait(self, step):
        for way, sign in ((0, -1), (1, 1)):
            ref = self.view(self.at(sign * step), self.rows(step == self.count // 2, way))
            self.copy(step, way, ref, ref).wait_recv()


class Gather(Line):
    def __init__(self, *args, slot):
        super().__init__(*args)
        self.slot = slot

    def start(self, step):
        for way, sign in ((0, 1), (1, -1)):
            rows = self.rows(step == 1, way)
            src = self.view(self.at(sign * (self.count // 2 + 1 - step)), rows)
            copy = self.copy(step, way, src, self.slot(way, step - 1, rows))
            copy.start()
            self.sent.append(copy)

    def add(self, step):
        for way, sign in ((0, 1), (1, -1)):
            rows = self.rows(step == 1, way)
            here = self.view(self.at(sign * (self.count // 2 - step)), rows)
            came = self.slot(way, step - 1, rows)
            self.copy(step, way, came, came).wait_recv()
            here[...] = (here[...].astype(jnp.float32) + came[...].astype(jnp.float32)).astype(
                here.dtype
            )


def counter():
    state = [0]

    def take(count):
        base = state[0]
        state[0] += count
        return base

    return take


def block_kernel(
    cut, x_ref, g_ref, up_ref, down_ref, mine_ref, gup_ref, gdown_ref,
    xs, gs, part, ra2, ra1, rb2, rb1, slope_of, hid, igr,
    own_sem, xsend, xrecv, gsend, grecv, rsend, rrecv,
):
    me = lax.axis_index("dp")
    e = lax.axis_index("expert")
    y, x = lax.div(me, NX), lax.rem(me, NX)
    width = x_ref.shape[1]
    lo, hi = pl.ds(0, cut), pl.ds(cut, width - cut)

    def device(yy, xx):
        return (lax.rem(yy + NY, NY) * NX + lax.rem(xx + NX, NX), e)

    xr, xl = device(y, x + 1), device(y, x - 1)
    yr, yl = device(y + 1, x), device(y - 1, x)

    barrier = pltpu.get_barrier_semaphore()
    for peer in (xr, xl, yr, yl):
        pl.semaphore_signal(barrier, inc=1, device_id=peer, device_id_type=MESH)
    pl.semaphore_wait(barrier, 4)

    owns = [
        pltpu.make_async_copy(x_ref, xs.at[y, x], own_sem.at[0]),
        pltpu.make_async_copy(g_ref, gs.at[y, x], own_sem.at[1]),
    ]
    for own in owns:
        own.start()
    for own in owns:
        own.wait()

    sent = []
    offsets = (0, 1, -1, 2, -2, 3, -3, 4)

    def row_of(offset):
        return lax.rem(y + offset + NY, NY)

    def gather_rounds(t, send_sem, recv_sem):
        take, sems = counter(), (send_sem, recv_sem)
        a1 = Spread(NX, x, lambda i, r: t.at[y, i, r, lo], xr, xl, sems, take, sent)
        a2 = Spread(NY, y, lambda i, r: t.at[i, :, r, lo], yr, yl, sems, take, sent)
        b1 = Spread(NY, y, lambda i, r: t.at[i, x, r, hi], yr, yl, sems, take, sent)
        b2 = {
            o: Spread(
                NX, x, (lambda yy: lambda i, r: t.at[yy, i, r, hi])(row_of(o)),
                xr, xl, sems, take, sent,
            )
            for o in offsets
        }

        def turn(*offs):
            for o in offs:
                b2[o].wait(1)
                b2[o].start(2)

        a1.start(1)
        b1.start(1)
        b2[0].start(1)
        yield
        b1.wait(1)
        b1.start(2)
        a1.wait(1)
        a1.start(2)
        b2[1].start(1)
        b2[-1].start(1)
        yield
        b1.wait(2)
        b1.start(3)
        a1.wait(2)
        a2.start(1)
        b2[2].start(1)
        b2[-2].start(1)
        turn(0)
        yield
        b1.wait(3)
        b1.start(4)
        b2[3].start(1)
        b2[-3].start(1)
        turn(1, -1)
        yield
        b1.wait(4)
        b2[4].start(1)
        a2.wait(1)
        a2.start(2)
        turn(2, -2)
        yield
        a2.wait(2)
        a2.start(3)
        turn(3, -3)
        yield
        a2.wait(3)
        a2.start(4)
        turn(4)
        yield
        for o in offsets:
            b2[o].wait(2)
        a2.wait(4)

    def sum_rounds():
        take, sems = counter(), (rsend, rrecv)
        a2 = Gather(
            NY, y, lambda i, r: part.at[i, :, r, lo], yr, yl, sems, take, sent,
            slot=lambda w, s, r: ra2.at[w, s, :, r, :],
        )
        a1 = Gather(
            NX, x, lambda i, r: part.at[y, i, r, lo], xr, xl, sems, take, sent,
            slot=lambda w, s, r: ra1.at[w, s, r, :],
        )
        b1 = Gather(
            NY, y, lambda i, r: part.at[i, x, r, hi], yr, yl, sems, take, sent,
            slot=lambda w, s, r: rb1.at[w, s, r, :],
        )
        b2 = {
            o: Gather(
                NX, x, (lambda yy: lambda i, r: part.at[yy, i, r, hi])(row_of(o)),
                xr, xl, sems, take, sent,
                slot=(lambda n: lambda w, s, r: rb2.at[n, w, s, r, :])(n),
            )
            for n, o in enumerate(offsets)
        }

        def turn(*offs):
            for o in offs:
                b2[o].add(1)
                b2[o].start(2)

        def done(*offs):
            for o in offs:
                b2[o].add(2)

        a2.start(1)
        for o in (4, 3, -3, 2, -2):
            b2[o].start(1)
        yield
        turn(4)
        a2.add(1)
        a2.start(2)
        turn(3, -3)
        for o in (1, -1, 0):
            b2[o].start(1)
        yield
        done(4)
        b1.start(1)
        turn(2, -2)
        yield
        a2.add(2)
        a2.start(3)
        done(3, -3)
        b1.add(1)
        b1.start(2)
        turn(1, -1, 0)
        yield
        a2.add(3)
        a2.start(4)
        done(2, -2)
        b1.add(2)
        b1.start(3)
        yield
        a2.add(4)
        a1.start(1)
        done(1, -1)
        b1.add(3)
        b1.start(4)
        yield
        a1.add(1)
        a1.start(2)
        done(0)
        yield
        b1.add(4)
        a1.add(2)

    nt = (((1,), (1,)), ((), ()))
    tn = (((0,), (0,)), ((), ()))
    chunk = NX * 32

    def forward(first, last):
        def body(c, carry):
            rows = xs[c].reshape(chunk, width)
            v = lax.dot_general(up_ref[...], rows, nt, preferred_element_type=jnp.float32)
            t = jnp.tanh(ROOT * (v + CUBE * v * v * v))
            columns = pl.ds(pl.multiple_of(c * chunk, chunk), chunk)
            slope_of[:, columns] = 0.5 * (1.0 + t) + 0.5 * v * (1.0 - t * t) * (
                ROOT * (1.0 + 3.0 * CUBE * v * v)
            )
            h = (0.5 * v * (1.0 + t)).astype(jnp.bfloat16)
            hid[:, columns] = h
            p = lax.dot_general(h, down_ref[...], tn, preferred_element_type=jnp.float32)
            part[c] = p.astype(jnp.bfloat16).reshape(NX, 32, width)
            return carry

        lax.fori_loop(first, last, body, 0)

    def backward():
        def body(c, carry):
            rows = gs[c].reshape(chunk, width)
            v = lax.dot_general(down_ref[...], rows, nt, preferred_element_type=jnp.float32)
            columns = pl.ds(pl.multiple_of(c * chunk, chunk), chunk)
            igr[:, columns] = (v * slope_of[:, columns]).astype(jnp.bfloat16)
            return carry

        lax.fori_loop(0, NY, body, 0)

    def weight_sums(left, t, out):
        tile = min(256, width)

        def body(j, carry):
            columns = pl.ds(pl.multiple_of(j * tile, tile), tile)
            rows = t[:, :, :, columns].reshape(NY * chunk, tile)
            out[:, columns] = jnp.dot(left[...], rows, preferred_element_type=jnp.float32)
            return carry

        lax.fori_loop(0, width // tile, body, 0)

    xg = gather_rounds(xs, xsend, xrecv)
    gg = gather_rounds(gs, gsend, grecv)
    for _ in range(4):
        next(xg)
    next(gg)
    next(xg)
    next(gg)
    next(xg)
    next(gg)
    next(xg)
    next(gg)
    next(xg, None)
    forward(0, NY // 2)
    next(gg)
    forward(NY // 2, NY)
    rg = sum_rounds()
    next(rg)
    next(gg)
    next(rg)
    next(gg)
    next(rg)
    next(gg, None)
    backward()
    next(rg)
    weight_sums(hid, gs, gdown_ref)
    next(rg)
    weight_sums(igr, xs, gup_ref)
    for _ in rg:
        pass
    mine_ref[...] = part[y, x]
    for copy in sent:
        copy.wait_send()


def block(rows, grads, up, down):
    n, width = rows.shape
    units = up.shape[0]
    cut = max(1, (width // 128) * 5 // 12) * 128
    rest = width - cut
    bf, f32 = jnp.bfloat16, jnp.float32
    vmem = pl.BlockSpec(memory_space=pltpu.VMEM)
    dma = lambda k: pltpu.SemaphoreType.DMA((k,))
    return pl.pallas_call(
        functools.partial(block_kernel, cut),
        out_shape=(
            jax.ShapeDtypeStruct((n, width), bf),
            jax.ShapeDtypeStruct((units, width), f32),
            jax.ShapeDtypeStruct((units, width), f32),
        ),
        in_specs=[vmem] * 4,
        out_specs=(vmem,) * 3,
        scratch_shapes=[
            pltpu.VMEM((NY, NX, n, width), bf),
            pltpu.VMEM((NY, NX, n, width), bf),
            pltpu.VMEM((NY, NX, n, width), bf),
            pltpu.VMEM((2, 4, NX, n, cut), bf),
            pltpu.VMEM((2, 2, n, cut), bf),
            pltpu.VMEM((8, 2, 2, n, rest), bf),
            pltpu.VMEM((2, 4, n, rest), bf),
            pltpu.VMEM((units, NY * NX * n), f32),
            pltpu.VMEM((units, NY * NX * n), bf),
            pltpu.VMEM((units, NY * NX * n), bf),
            dma(2),
        ]
        + [dma(SEMS)] * 6,
        compiler_params=pltpu.CompilerParams(
            collective_id=0, has_side_effects=True, vmem_limit_bytes=58 * 1024 * 1024
        ),
    )(rows, grads, up, down)


def local(features, classes, live_counts, cotangent, up_weight, down_weight):
    expert_count = lax.axis_size("expert")
    row_count, width = features.shape
    span = row_count // expert_count
    own_table = slot_table(classes, live_counts[0], span, expert_count)
    both = jnp.concatenate([features, cotangent], axis=1)
    send = jnp.dot(own_table, both, preferred_element_type=jnp.float32).astype(jnp.bfloat16)
    send = send.reshape(expert_count, span, 2 * width)
    came = lax.all_to_all(send, "expert", split_axis=0, concat_axis=0, tiled=True)
    came = came.reshape(row_count, 2 * width)
    mine, grad_up, grad_down = block(
        came[:, :width], came[:, width:], up_weight[0], down_weight[0]
    )
    back = mine.reshape(expert_count, span, width)
    back = lax.all_to_all(back, "expert", split_axis=0, concat_axis=0, tiled=True)
    mixed = jnp.dot(
        own_table.T, back.reshape(row_count, width), preferred_element_type=jnp.float32
    ).astype(jnp.bfloat16)
    return (mixed, grad_up[None], grad_down[None])


def solution(mesh):
    placed = (
        P(("dp", "expert"), None),
        P(("dp", "expert")),
        P(("dp", "expert")),
        P(("dp", "expert"), None),
        P("expert", "dp", None),
        P("expert", "dp", None),
    )
    return jax.shard_map(
        local,
        mesh=mesh,
        in_specs=placed,
        out_specs=(P(("dp", "expert"), None), P("expert", "dp", None), P("expert", "dp", None)),
        check_vma=False,
    )
```

```python
import functools

import jax
import jax.numpy as jnp
from jax import lax
from jax.experimental import pallas as pl
from jax.experimental.pallas import tpu as pltpu
from jax.sharding import PartitionSpec as P

NY, NX = 8, 4
MESH = pl.DeviceIdType.MESH
SEMS = 52
PAD = 8
ROOT = 0.7978845608028654
CUBE = 0.044715


def slot_table(group_classes, group_counts, expert_count):
    row_count = group_classes.shape[0]
    position = lax.broadcasted_iota(jnp.int32, (1, row_count), 1)
    live = position < group_counts
    same = group_classes[:, None] == group_classes[None, :]
    later = lax.broadcasted_iota(jnp.int32, (row_count, row_count), 0)
    sooner = lax.broadcasted_iota(jnp.int32, (row_count, row_count), 1)
    place = jnp.sum((same & (sooner < later)).astype(jnp.int32), axis=1)
    target = group_classes * PAD + place
    slots = lax.broadcasted_iota(jnp.int32, (expert_count * PAD, 1), 0)
    chosen = (target[None, :] == slots) & live
    return chosen.astype(jnp.bfloat16)


class Line:
    def __init__(self, count, here, view, right, left, sems, take, sent):
        self.count, self.here, self.view = count, here, view
        self.right, self.left = right, left
        self.send_sem, self.recv_sem = sems
        self.base = take(count)
        self.sent = sent

    def at(self, offset):
        return lax.rem(self.here + offset + self.count, self.count)

    def rows(self, half, way):
        rows = 32
        if not half:
            return pl.ds(0, rows)
        return pl.ds(0, rows // 2) if way == 0 else pl.ds(rows // 2, rows // 2)

    def copy(self, step, way, src, dst):
        k = self.base + 2 * (step - 1) + way
        return pltpu.make_async_remote_copy(
            src_ref=src,
            dst_ref=dst,
            send_sem=self.send_sem.at[k],
            recv_sem=self.recv_sem.at[k],
            device_id=self.right if way == 0 else self.left,
            device_id_type=MESH,
        )


class Spread(Line):
    def start(self, step):
        for way, sign in ((0, -1), (1, 1)):
            ref = self.view(self.at(sign * (step - 1)), self.rows(step == self.count // 2, way))
            copy = self.copy(step, way, ref, ref)
            copy.start()
            self.sent.append(copy)

    def wait(self, step):
        for way, sign in ((0, -1), (1, 1)):
            ref = self.view(self.at(sign * step), self.rows(step == self.count // 2, way))
            self.copy(step, way, ref, ref).wait_recv()


class Gather(Line):
    def __init__(self, *args, slot):
        super().__init__(*args)
        self.slot = slot

    def start(self, step):
        for way, sign in ((0, 1), (1, -1)):
            rows = self.rows(step == 1, way)
            src = self.view(self.at(sign * (self.count // 2 + 1 - step)), rows)
            copy = self.copy(step, way, src, self.slot(way, step - 1, rows))
            copy.start()
            self.sent.append(copy)

    def add(self, step):
        for way, sign in ((0, 1), (1, -1)):
            rows = self.rows(step == 1, way)
            here = self.view(self.at(sign * (self.count // 2 - step)), rows)
            came = self.slot(way, step - 1, rows)
            self.copy(step, way, came, came).wait_recv()
            here[...] = (here[...].astype(jnp.float32) + came[...].astype(jnp.float32)).astype(
                here.dtype
            )


def counter():
    state = [0]

    def take(count):
        base = state[0]
        state[0] += count
        return base

    return take


def block_kernel(
    cut, experts, table_ref, x_ref, g_ref, up_ref, down_ref, mixed_ref, gup_ref, gdown_ref,
    xs, gs, part, ra2, ra1, rb2, rb1, slope_of, hid, igr, out_to, in_from, wide,
    own_sem, dsend, drecv, xsend, xrecv, gsend, grecv, rsend, rrecv,
):
    me = lax.axis_index("dp")
    e = lax.axis_index("expert")
    y, x = lax.div(me, NX), lax.rem(me, NX)
    width = x_ref.shape[1]
    lo, hi = pl.ds(0, cut), pl.ds(cut, width - cut)

    def device(yy, xx):
        return (lax.rem(yy + NY, NY) * NX + lax.rem(xx + NX, NX), e)

    xr, xl = device(y, x + 1), device(y, x - 1)
    yr, yl = device(y + 1, x), device(y - 1, x)

    n = x_ref.shape[0]
    span = n // experts

    def other(offset):
        return lax.rem(e + offset + experts, experts)

    barrier = pltpu.get_barrier_semaphore()
    for peer in [xr, xl, yr, yl] + [(me, other(d)) for d in range(1, experts)]:
        pl.semaphore_signal(barrier, inc=1, device_id=peer, device_id_type=MESH)

    def exchange(k, d, way):
        there = other(d * way)
        return pltpu.make_async_remote_copy(
            src_ref=out_to.at[k, there],
            dst_ref=in_from.at[k, e if way == 1 else there],
            send_sem=dsend.at[k, d],
            recv_sem=drecv.at[k, d],
            device_id=(me, there),
            device_id_type=MESH,
        )

    def own(k):
        return pltpu.make_async_copy(out_to.at[k, e], in_from.at[k, e], own_sem.at[k])

    near = [d for h in range(1, experts // 2 + 1) for d in sorted({h, experts - h})]

    def fill(k, table, rows):
        spread = jnp.dot(table, rows, preferred_element_type=jnp.float32)
        out_to[k] = spread.reshape(experts, PAD, width)[:, :span, :].astype(jnp.bfloat16)

    def leave(k):
        own(k).start()
        for d in near:
            copy = exchange(k, d, 1)
            copy.start()
            sent.append(copy)

    def arrive(k, table):
        own(k).wait()
        for d in near:
            exchange(k, d, -1).wait_recv()
        wide[:, :span, :] = in_from[k].astype(jnp.float32)
        flat = wide[...].reshape(experts * PAD, width).astype(jnp.bfloat16)
        return lax.dot_general(
            table, flat, (((0,), (0,)), ((), ())), preferred_element_type=jnp.float32
        ).astype(jnp.bfloat16)

    wide[...] = jnp.zeros_like(wide)
    slot = lax.broadcasted_iota(jnp.int32, (experts * PAD, n), 0)
    row = lax.broadcasted_iota(jnp.int32, (experts * PAD, n), 1)
    dense = (slot == lax.div(row, span) * PAD + lax.rem(row, span)).astype(jnp.bfloat16)
    sent = []
    fill(0, table_ref[...], x_ref[...])
    pl.semaphore_wait(barrier, 3 + experts)
    leave(0)
    fill(1, table_ref[...], g_ref[...])
    leave(1)
    xs[y, x] = arrive(0, dense)

    offsets = (0, 1, -1, 2, -2, 3, -3, 4)

    def row_of(offset):
        return lax.rem(y + offset + NY, NY)

    def gather_rounds(t, send_sem, recv_sem):
        take, sems = counter(), (send_sem, recv_sem)
        a1 = Spread(NX, x, lambda i, r: t.at[y, i, r, lo], xr, xl, sems, take, sent)
        a2 = Spread(NY, y, lambda i, r: t.at[i, :, r, lo], yr, yl, sems, take, sent)
        b1 = Spread(NY, y, lambda i, r: t.at[i, x, r, hi], yr, yl, sems, take, sent)
        b2 = {
            o: Spread(
                NX, x, (lambda yy: lambda i, r: t.at[yy, i, r, hi])(row_of(o)),
                xr, xl, sems, take, sent,
            )
            for o in offsets
        }

        def turn(*offs):
            for o in offs:
                b2[o].wait(1)
                b2[o].start(2)

        a1.start(1)
        b1.start(1)
        b2[0].start(1)
        yield
        b1.wait(1)
        b1.start(2)
        a1.wait(1)
        a1.start(2)
        b2[1].start(1)
        b2[-1].start(1)
        yield
        b1.wait(2)
        b1.start(3)
        a1.wait(2)
        a2.start(1)
        b2[2].start(1)
        b2[-2].start(1)
        turn(0)
        yield
        b1.wait(3)
        b1.start(4)
        b2[3].start(1)
        b2[-3].start(1)
        turn(1, -1)
        yield
        b1.wait(4)
        b2[4].start(1)
        a2.wait(1)
        a2.start(2)
        turn(2, -2)
        yield
        a2.wait(2)
        a2.start(3)
        turn(3, -3)
        yield
        a2.wait(3)
        a2.start(4)
        turn(4)
        yield
        for o in offsets:
            b2[o].wait(2)
        a2.wait(4)

    def sum_rounds():
        take, sems = counter(), (rsend, rrecv)
        a2 = Gather(
            NY, y, lambda i, r: part.at[i, :, r, lo], yr, yl, sems, take, sent,
            slot=lambda w, s, r: ra2.at[w, s, :, r, :],
        )
        a1 = Gather(
            NX, x, lambda i, r: part.at[y, i, r, lo], xr, xl, sems, take, sent,
            slot=lambda w, s, r: ra1.at[w, s, r, :],
        )
        b1 = Gather(
            NY, y, lambda i, r: part.at[i, x, r, hi], yr, yl, sems, take, sent,
            slot=lambda w, s, r: rb1.at[w, s, r, :],
        )
        b2 = {
            o: Gather(
                NX, x, (lambda yy: lambda i, r: part.at[yy, i, r, hi])(row_of(o)),
                xr, xl, sems, take, sent,
                slot=(lambda n: lambda w, s, r: rb2.at[n, w, s, r, :])(n),
            )
            for n, o in enumerate(offsets)
        }

        def turn(*offs):
            for o in offs:
                b2[o].add(1)
                b2[o].start(2)

        def done(*offs):
            for o in offs:
                b2[o].add(2)

        a2.start(1)
        for o in (4, 3, -3, 2, -2):
            b2[o].start(1)
        yield
        turn(4)
        a2.add(1)
        a2.start(2)
        turn(3, -3)
        for o in (1, -1, 0):
            b2[o].start(1)
        yield
        done(4)
        b1.start(1)
        turn(2, -2)
        yield
        a2.add(2)
        a2.start(3)
        done(3, -3)
        b1.add(1)
        b1.start(2)
        turn(1, -1, 0)
        yield
        a2.add(3)
        a2.start(4)
        done(2, -2)
        b1.add(2)
        b1.start(3)
        yield
        a2.add(4)
        a1.start(1)
        done(1, -1)
        b1.add(3)
        b1.start(4)
        yield
        a1.add(1)
        a1.start(2)
        done(0)
        yield
        b1.add(4)
        a1.add(2)

    nt = (((1,), (1,)), ((), ()))
    tn = (((0,), (0,)), ((), ()))
    chunk = NX * 32

    def forward(first, last):
        def body(c, carry):
            rows = xs[c].reshape(chunk, width)
            v = lax.dot_general(up_ref[...], rows, nt, preferred_element_type=jnp.float32)
            t = jnp.tanh(ROOT * (v + CUBE * v * v * v))
            columns = pl.ds(pl.multiple_of(c * chunk, chunk), chunk)
            slope_of[:, columns] = 0.5 * (1.0 + t) + 0.5 * v * (1.0 - t * t) * (
                ROOT * (1.0 + 3.0 * CUBE * v * v)
            )
            h = (0.5 * v * (1.0 + t)).astype(jnp.bfloat16)
            hid[:, columns] = h
            p = lax.dot_general(h, down_ref[...], tn, preferred_element_type=jnp.float32)
            part[c] = p.astype(jnp.bfloat16).reshape(NX, 32, width)
            return carry

        lax.fori_loop(first, last, body, 0)

    def backward():
        def body(c, carry):
            rows = gs[c].reshape(chunk, width)
            v = lax.dot_general(down_ref[...], rows, nt, preferred_element_type=jnp.float32)
            columns = pl.ds(pl.multiple_of(c * chunk, chunk), chunk)
            igr[:, columns] = (v * slope_of[:, columns]).astype(jnp.bfloat16)
            return carry

        lax.fori_loop(0, NY, body, 0)

    def weight_sums(left, t, out):
        tile = min(256, width)

        def body(j, carry):
            columns = pl.ds(pl.multiple_of(j * tile, tile), tile)
            rows = t[:, :, :, columns].reshape(NY * chunk, tile)
            out[:, columns] = jnp.dot(left[...], rows, preferred_element_type=jnp.float32)
            return carry

        lax.fori_loop(0, width // tile, body, 0)

    xg = gather_rounds(xs, xsend, xrecv)
    gg = gather_rounds(gs, gsend, grecv)
    for _ in range(2):
        next(xg)
    gs[y, x] = arrive(1, dense)
    for _ in range(2):
        next(xg)
    next(gg)
    next(xg)
    next(gg)
    next(xg)
    next(gg)
    next(xg)
    next(gg)
    next(xg, None)
    forward(0, NY // 2)
    next(gg)
    forward(NY // 2, NY)
    rg = sum_rounds()
    next(rg)
    next(gg)
    next(rg)
    next(gg)
    next(rg)
    next(gg, None)
    backward()
    next(rg)
    weight_sums(hid, gs, gdown_ref)
    next(rg)
    weight_sums(igr, xs, gup_ref)
    for _ in rg:
        pass
    fill(2, dense, part[y, x])
    leave(2)
    mixed_ref[...] = arrive(2, table_ref[...])
    for copy in sent:
        copy.wait_send()


def block(table, rows, grads, up, down, experts):
    n, width = rows.shape
    units = up.shape[0]
    cut = max(1, (width // 128) * 5 // 12) * 128
    rest = width - cut
    bf, f32 = jnp.bfloat16, jnp.float32
    vmem = pl.BlockSpec(memory_space=pltpu.VMEM)
    dma = lambda k: pltpu.SemaphoreType.DMA((k,))
    return pl.pallas_call(
        functools.partial(block_kernel, cut, experts),
        out_shape=(
            jax.ShapeDtypeStruct((n, width), bf),
            jax.ShapeDtypeStruct((units, width), f32),
            jax.ShapeDtypeStruct((units, width), f32),
        ),
        in_specs=[vmem] * 5,
        out_specs=(vmem,) * 3,
        scratch_shapes=[
            pltpu.VMEM((NY, NX, n, width), bf),
            pltpu.VMEM((NY, NX, n, width), bf),
            pltpu.VMEM((NY, NX, n, width), bf),
            pltpu.VMEM((2, 4, NX, n, cut), bf),
            pltpu.VMEM((2, 2, n, cut), bf),
            pltpu.VMEM((8, 2, 2, n, rest), bf),
            pltpu.VMEM((2, 4, n, rest), bf),
            pltpu.VMEM((units, NY * NX * n), f32),
            pltpu.VMEM((units, NY * NX * n), bf),
            pltpu.VMEM((units, NY * NX * n), bf),
            pltpu.VMEM((3, experts, n // experts, width), bf),
            pltpu.VMEM((3, experts, n // experts, width), bf),
            pltpu.VMEM((experts, PAD, width), f32),
            dma(3),
            pltpu.SemaphoreType.DMA((3, experts)),
            pltpu.SemaphoreType.DMA((3, experts)),
        ]
        + [dma(SEMS)] * 6,
        compiler_params=pltpu.CompilerParams(
            collective_id=0, has_side_effects=True, vmem_limit_bytes=58 * 1024 * 1024
        ),
    )(table, rows, grads, up, down)


def local(features, classes, live_counts, cotangent, up_weight, down_weight):
    expert_count = lax.axis_size("expert")
    table = slot_table(classes, live_counts[0], expert_count)
    mixed, grad_up, grad_down = block(
        table, features, cotangent, up_weight[0], down_weight[0], expert_count
    )
    return (mixed, grad_up[None], grad_down[None])


def solution(mesh):
    placed = (
        P(("dp", "expert"), None),
        P(("dp", "expert")),
        P(("dp", "expert")),
        P(("dp", "expert"), None),
        P("expert", "dp", None),
        P("expert", "dp", None),
    )
    return jax.shard_map(
        local,
        mesh=mesh,
        in_specs=placed,
        out_specs=(P(("dp", "expert"), None), P("expert", "dp", None), P("expert", "dp", None)),
        check_vma=False,
    )
```

```python
import functools

import jax
import jax.numpy as jnp
from jax import lax
from jax.experimental import pallas as pl
from jax.experimental.pallas import tpu as pltpu
from jax.sharding import PartitionSpec as P

NY, NX = 8, 4
MESH = pl.DeviceIdType.MESH
SEMS = 76
PAD = 8
ROOT = 0.7978845608028654
CUBE = 0.044715


def slot_table(group_classes, group_counts, expert_count):
    row_count = group_classes.shape[0]
    position = lax.broadcasted_iota(jnp.int32, (1, row_count), 1)
    live = position < group_counts
    same = group_classes[:, None] == group_classes[None, :]
    later = lax.broadcasted_iota(jnp.int32, (row_count, row_count), 0)
    sooner = lax.broadcasted_iota(jnp.int32, (row_count, row_count), 1)
    place = jnp.sum((same & (sooner < later)).astype(jnp.int32), axis=1)
    target = group_classes * PAD + place
    slots = lax.broadcasted_iota(jnp.int32, (expert_count * PAD, 1), 0)
    chosen = (target[None, :] == slots) & live
    return chosen.astype(jnp.bfloat16)


class Line:
    def __init__(self, count, here, view, right, left, sems, take, sent):
        self.count, self.here, self.view = count, here, view
        self.right, self.left = right, left
        self.send_sem, self.recv_sem = sems
        self.base = take(count)
        self.sent = sent

    def at(self, offset):
        return lax.rem(self.here + offset + self.count, self.count)

    def rows(self, half, way):
        rows = 32
        if not half:
            return pl.ds(0, rows)
        return pl.ds(0, rows // 2) if way == 0 else pl.ds(rows // 2, rows // 2)

    def copy(self, step, way, src, dst):
        k = self.base + 2 * (step - 1) + way
        return pltpu.make_async_remote_copy(
            src_ref=src,
            dst_ref=dst,
            send_sem=self.send_sem.at[k],
            recv_sem=self.recv_sem.at[k],
            device_id=self.right if way == 0 else self.left,
            device_id_type=MESH,
        )


class Spread(Line):
    def start(self, step):
        for way, sign in ((0, -1), (1, 1)):
            ref = self.view(self.at(sign * (step - 1)), self.rows(step == self.count // 2, way))
            copy = self.copy(step, way, ref, ref)
            copy.start()
            self.sent.append(copy)

    def wait(self, step):
        for way, sign in ((0, -1), (1, 1)):
            ref = self.view(self.at(sign * step), self.rows(step == self.count // 2, way))
            self.copy(step, way, ref, ref).wait_recv()


class Gather(Line):
    def __init__(self, *args, slot):
        super().__init__(*args)
        self.slot = slot

    def start(self, step):
        for way, sign in ((0, 1), (1, -1)):
            rows = self.rows(step == 1, way)
            src = self.view(self.at(sign * (self.count // 2 + 1 - step)), rows)
            copy = self.copy(step, way, src, self.slot(way, step - 1, rows))
            copy.start()
            self.sent.append(copy)

    def add(self, step):
        for way, sign in ((0, 1), (1, -1)):
            rows = self.rows(step == 1, way)
            here = self.view(self.at(sign * (self.count // 2 - step)), rows)
            came = self.slot(way, step - 1, rows)
            self.copy(step, way, came, came).wait_recv()
            here[...] = (here[...].astype(jnp.float32) + came[...].astype(jnp.float32)).astype(
                here.dtype
            )


def counter():
    state = [0]

    def take(count):
        base = state[0]
        state[0] += count
        return base

    return take


def block_kernel(
    cut, experts, table_ref, x_ref, g_ref, up_ref, down_ref, mixed_ref, gup_ref, gdown_ref,
    xs, gs, part, ra2, ra1, rb2, rb1, slope_of, hid, igr, out_to, in_from, wide,
    own_sem, dsend, drecv, xsend, xrecv, gsend, grecv, rsend, rrecv,
):
    me = lax.axis_index("dp")
    e = lax.axis_index("expert")
    y, x = lax.div(me, NX), lax.rem(me, NX)
    width = x_ref.shape[1]
    lo, hi = pl.ds(0, cut), pl.ds(cut, width - cut)

    def device(yy, xx):
        return (lax.rem(yy + NY, NY) * NX + lax.rem(xx + NX, NX), e)

    xr, xl = device(y, x + 1), device(y, x - 1)
    yr, yl = device(y + 1, x), device(y - 1, x)

    n = x_ref.shape[0]
    span = n // experts

    def other(offset):
        return lax.rem(e + offset + experts, experts)

    barrier = pltpu.get_barrier_semaphore()
    for peer in [xr, xl, yr, yl] + [(me, other(d)) for d in range(1, experts)]:
        pl.semaphore_signal(barrier, inc=1, device_id=peer, device_id_type=MESH)

    def exchange(k, d, way):
        there = other(d * way)
        return pltpu.make_async_remote_copy(
            src_ref=out_to.at[k, there],
            dst_ref=in_from.at[k, e if way == 1 else there],
            send_sem=dsend.at[k, d],
            recv_sem=drecv.at[k, d],
            device_id=(me, there),
            device_id_type=MESH,
        )

    def own(k):
        return pltpu.make_async_copy(out_to.at[k, e], in_from.at[k, e], own_sem.at[k])

    near = [d for h in range(1, experts // 2 + 1) for d in sorted({h, experts - h})]

    def fill(k, table, rows):
        spread = jnp.dot(table, rows, preferred_element_type=jnp.float32)
        out_to[k] = spread.reshape(experts, PAD, width)[:, :span, :].astype(jnp.bfloat16)

    def leave(k):
        own(k).start()
        for d in near:
            copy = exchange(k, d, 1)
            copy.start()
            sent.append(copy)

    def arrive(k, table):
        own(k).wait()
        for d in near:
            exchange(k, d, -1).wait_recv()
        wide[:, :span, :] = in_from[k].astype(jnp.float32)
        flat = wide[...].reshape(experts * PAD, width).astype(jnp.bfloat16)
        return lax.dot_general(
            table, flat, (((0,), (0,)), ((), ())), preferred_element_type=jnp.float32
        ).astype(jnp.bfloat16)

    wide[...] = jnp.zeros_like(wide)
    slot = lax.broadcasted_iota(jnp.int32, (experts * PAD, n), 0)
    row = lax.broadcasted_iota(jnp.int32, (experts * PAD, n), 1)
    dense = (slot == lax.div(row, span) * PAD + lax.rem(row, span)).astype(jnp.bfloat16)
    sent = []
    fill(0, table_ref[...], x_ref[...])
    pl.semaphore_wait(barrier, 3 + experts)
    leave(0)
    fill(1, table_ref[...], g_ref[...])
    leave(1)
    xs[y, x] = arrive(0, dense)

    offsets = (0, 1, -1, 2, -2, 3, -3, 4)

    def row_of(offset):
        return lax.rem(y + offset + NY, NY)

    across = (0, 1, -1, 2)

    def column_of(offset):
        return lax.rem(x + offset + NX, NX)

    def gather_rounds(t, send_sem, recv_sem, ready):
        take, sems = counter(), (send_sem, recv_sem)
        a1 = Spread(NX, x, lambda i, r: t.at[y, i, r, lo], xr, xl, sems, take, sent)
        a2 = {
            o: Spread(
                NY, y, (lambda xx: lambda i, r: t.at[i, xx, r, lo])(column_of(o)),
                yr, yl, sems, take, sent,
            )
            for o in across
        }
        b1 = Spread(NY, y, lambda i, r: t.at[i, x, r, hi], yr, yl, sems, take, sent)
        b2 = {
            o: Spread(
                NX, x, (lambda yy: lambda i, r: t.at[yy, i, r, hi])(row_of(o)),
                xr, xl, sems, take, sent,
            )
            for o in offsets
        }

        def turn(*offs):
            for o in offs:
                b2[o].wait(1)
                b2[o].start(2)

        def relay(step, *offs):
            for o in offs:
                a2[o].wait(step)
                a2[o].start(step + 1)

        def whole(*offs):
            for o in offs:
                b2[o].wait(2)
                ready(o)

        a1.start(1)
        b1.start(1)
        a2[0].start(1)
        b2[0].start(1)
        yield
        b1.wait(1)
        b1.start(2)
        a1.wait(1)
        a1.start(2)
        for o in (1, -1):
            a2[o].start(1)
            b2[o].start(1)
        yield
        b1.wait(2)
        b1.start(3)
        b2[2].start(1)
        b2[-2].start(1)
        relay(1, 0)
        a1.wait(2)
        a2[2].start(1)
        turn(0)
        yield
        b1.wait(3)
        b1.start(4)
        b2[3].start(1)
        b2[-3].start(1)
        relay(1, 1, -1)
        turn(1, -1)
        yield
        b1.wait(4)
        b2[4].start(1)
        relay(2, 0)
        relay(1, 2)
        turn(2, -2)
        yield
        relay(2, 1, -1)
        turn(3, -3)
        relay(3, 0)
        relay(2, 2)
        whole(0)
        yield
        relay(3, 1, -1)
        turn(4)
        relay(3, 2)
        whole(1, -1)
        yield
        whole(2, -2)
        yield
        whole(3, -3)
        yield
        for o in across:
            a2[o].wait(4)
        whole(4)

    def sum_rounds():
        take, sems = counter(), (rsend, rrecv)
        a2 = {
            o: Gather(
                NY, y, (lambda xx: lambda i, r: part.at[i, xx, r, lo])(column_of(o)),
                yr, yl, sems, take, sent,
                slot=(lambda m: lambda w, s, r: ra2.at[m, w, s, r, :])(m),
            )
            for m, o in enumerate(across)
        }
        a1 = Gather(
            NX, x, lambda i, r: part.at[y, i, r, lo], xr, xl, sems, take, sent,
            slot=lambda w, s, r: ra1.at[w, s, r, :],
        )
        b1 = Gather(
            NY, y, lambda i, r: part.at[i, x, r, hi], yr, yl, sems, take, sent,
            slot=lambda w, s, r: rb1.at[w, s, r, :],
        )
        b2 = {
            o: Gather(
                NX, x, (lambda yy: lambda i, r: part.at[yy, i, r, hi])(row_of(o)),
                xr, xl, sems, take, sent,
                slot=(lambda m: lambda w, s, r: rb2.at[m, w, s, r, :])(m),
            )
            for m, o in enumerate(offsets)
        }

        def turn(*offs):
            for o in offs:
                b2[o].add(1)
                b2[o].start(2)

        def relay(step, *offs):
            for o in offs:
                a2[o].add(step)
                a2[o].start(step + 1)

        def done(*offs):
            for o in offs:
                b2[o].add(2)

        b2[4].start(1)
        a2[2].start(1)
        for o in (1, -1):
            a2[o].start(1)
            b2[3 * o].start(1)
        a2[0].start(1)
        b2[2].start(1)
        b2[-2].start(1)
        yield
        turn(4)
        relay(1, 2)
        turn(3, -3)
        relay(1, 1, -1, 0)
        for o in (1, -1, 0):
            b2[o].start(1)
        yield
        done(4)
        b1.start(1)
        relay(2, 2)
        turn(2, -2)
        relay(2, 1, -1)
        yield
        done(3, -3)
        b1.add(1)
        b1.start(2)
        relay(2, 0)
        relay(3, 2)
        turn(1, -1, 0)
        yield
        relay(3, 1, -1)
        done(2, -2)
        b1.add(2)
        b1.start(3)
        relay(3, 0)
        a2[2].add(4)
        a1.start(1)
        yield
        done(1, -1)
        b1.add(3)
        b1.start(4)
        a2[1].add(4)
        a2[-1].add(4)
        a1.add(1)
        a1.start(2)
        yield
        a2[0].add(4)
        done(0)
        b1.add(4)
        a1.add(2)

    nt = (((1,), (1,)), ((), ()))
    tn = (((0,), (0,)), ((), ()))
    chunk = NX * 32

    def forward(offset):
        c = row_of(offset)
        rows = xs[c].reshape(chunk, width)
        v = lax.dot_general(up_ref[...], rows, nt, preferred_element_type=jnp.float32)
        t = jnp.tanh(ROOT * (v + CUBE * v * v * v))
        columns = pl.ds(pl.multiple_of(c * chunk, chunk), chunk)
        slope_of[:, columns] = 0.5 * (1.0 + t) + 0.5 * v * (1.0 - t * t) * (
            ROOT * (1.0 + 3.0 * CUBE * v * v)
        )
        h = (0.5 * v * (1.0 + t)).astype(jnp.bfloat16)
        hid[:, columns] = h
        p = lax.dot_general(h, down_ref[...], tn, preferred_element_type=jnp.float32)
        part[c] = p.astype(jnp.bfloat16).reshape(NX, 32, width)

    def backward(offset):
        c = row_of(offset)
        rows = gs[c].reshape(chunk, width)
        v = lax.dot_general(down_ref[...], rows, nt, preferred_element_type=jnp.float32)
        columns = pl.ds(pl.multiple_of(c * chunk, chunk), chunk)
        igr[:, columns] = (v * slope_of[:, columns]).astype(jnp.bfloat16)

    def weight_sums(left, t, out):
        tile = min(256, width)

        def body(j, carry):
            columns = pl.ds(pl.multiple_of(j * tile, tile), tile)
            rows = t[:, :, :, columns].reshape(NY * chunk, tile)
            out[:, columns] = jnp.dot(left[...], rows, preferred_element_type=jnp.float32)
            return carry

        lax.fori_loop(0, width // tile, body, 0)

    xg = gather_rounds(xs, xsend, xrecv, forward)
    gg = gather_rounds(gs, gsend, grecv, backward)
    rg = sum_rounds()
    for _ in range(3):
        next(xg)
    gs[y, x] = arrive(1, dense)
    for _ in range(2):
        next(xg)
    for _ in range(4):
        next(gg)
        next(xg)
    next(gg)
    next(xg, None)
    for _ in range(5):
        next(rg)
        next(gg, None)
    weight_sums(hid, gs, gdown_ref)
    next(rg)
    weight_sums(igr, xs, gup_ref)
    next(rg, None)
    fill(2, dense, part[y, x])
    leave(2)
    mixed_ref[...] = arrive(2, table_ref[...])
    for copy in sent:
        copy.wait_send()


def block(table, rows, grads, up, down, experts):
    n, width = rows.shape
    units = up.shape[0]
    cut = max(1, (width // 128) * 5 // 12) * 128
    rest = width - cut
    bf, f32 = jnp.bfloat16, jnp.float32
    vmem = pl.BlockSpec(memory_space=pltpu.VMEM)
    dma = lambda k: pltpu.SemaphoreType.DMA((k,))
    return pl.pallas_call(
        functools.partial(block_kernel, cut, experts),
        out_shape=(
            jax.ShapeDtypeStruct((n, width), bf),
            jax.ShapeDtypeStruct((units, width), f32),
            jax.ShapeDtypeStruct((units, width), f32),
        ),
        in_specs=[vmem] * 5,
        out_specs=(vmem,) * 3,
        scratch_shapes=[
            pltpu.VMEM((NY, NX, n, width), bf),
            pltpu.VMEM((NY, NX, n, width), bf),
            pltpu.VMEM((NY, NX, n, width), bf),
            pltpu.VMEM((NX, 2, 4, n, cut), bf),
            pltpu.VMEM((2, 2, n, cut), bf),
            pltpu.VMEM((8, 2, 2, n, rest), bf),
            pltpu.VMEM((2, 4, n, rest), bf),
            pltpu.VMEM((units, NY * NX * n), f32),
            pltpu.VMEM((units, NY * NX * n), bf),
            pltpu.VMEM((units, NY * NX * n), bf),
            pltpu.VMEM((3, experts, n // experts, width), bf),
            pltpu.VMEM((3, experts, n // experts, width), bf),
            pltpu.VMEM((experts, PAD, width), f32),
            dma(3),
            pltpu.SemaphoreType.DMA((3, experts)),
            pltpu.SemaphoreType.DMA((3, experts)),
        ]
        + [dma(SEMS)] * 6,
        compiler_params=pltpu.CompilerParams(
            collective_id=0, has_side_effects=True, vmem_limit_bytes=58 * 1024 * 1024
        ),
    )(table, rows, grads, up, down)


def local(features, classes, live_counts, cotangent, up_weight, down_weight):
    expert_count = lax.axis_size("expert")
    table = slot_table(classes, live_counts[0], expert_count)
    mixed, grad_up, grad_down = block(
        table, features, cotangent, up_weight[0], down_weight[0], expert_count
    )
    return (mixed, grad_up[None], grad_down[None])


def solution(mesh):
    placed = (
        P(("dp", "expert"), None),
        P(("dp", "expert")),
        P(("dp", "expert")),
        P(("dp", "expert"), None),
        P("expert", "dp", None),
        P("expert", "dp", None),
    )
    return jax.shard_map(
        local,
        mesh=mesh,
        in_specs=placed,
        out_specs=(P(("dp", "expert"), None), P("expert", "dp", None), P("expert", "dp", None)),
        check_vma=False,
    )
```

```python
import functools

import jax
import jax.numpy as jnp
from jax import lax
from jax.experimental import pallas as pl
from jax.experimental.pallas import tpu as pltpu
from jax.sharding import PartitionSpec as P

NY, NX = 8, 4
MESH = pl.DeviceIdType.MESH
SEMS = 76
PAD = 8
ROOT = 0.7978845608028654
CUBE = 0.044715


def slot_table(labels, live, experts):
    count = labels.shape[1]
    across = jnp.broadcast_to(labels, (count, count)).astype(jnp.float32)
    down = across.T
    sooner = lax.broadcasted_iota(jnp.int32, (count, count), 0)
    later = lax.broadcasted_iota(jnp.int32, (count, count), 1)
    earlier = jnp.where((across == down) & (sooner < later), 1.0, 0.0)
    place = jnp.sum(earlier, axis=0, keepdims=True).astype(jnp.int32)
    position = lax.broadcasted_iota(jnp.int32, (1, count), 1)
    target = jnp.where(position < live, labels * PAD + place, -1)
    slots = lax.broadcasted_iota(jnp.int32, (experts * PAD, count), 0)
    return jnp.where(slots == target, 1.0, 0.0).astype(jnp.bfloat16)


class Line:
    def __init__(self, count, here, view, right, left, sems, take, sent):
        self.count, self.here, self.view = count, here, view
        self.right, self.left = right, left
        self.send_sem, self.recv_sem = sems
        self.base = take(count)
        self.sent = sent

    def at(self, offset):
        return lax.rem(self.here + offset + self.count, self.count)

    def rows(self, half, way):
        rows = 32
        if not half:
            return pl.ds(0, rows)
        return pl.ds(0, rows // 2) if way == 0 else pl.ds(rows // 2, rows // 2)

    def copy(self, step, way, src, dst):
        k = self.base + 2 * (step - 1) + way
        return pltpu.make_async_remote_copy(
            src_ref=src,
            dst_ref=dst,
            send_sem=self.send_sem.at[k],
            recv_sem=self.recv_sem.at[k],
            device_id=self.right if way == 0 else self.left,
            device_id_type=MESH,
        )


class Spread(Line):
    def start(self, step):
        for way, sign in ((0, -1), (1, 1)):
            ref = self.view(self.at(sign * (step - 1)), self.rows(step == self.count // 2, way))
            copy = self.copy(step, way, ref, ref)
            copy.start()
            self.sent.append(copy)

    def wait(self, step):
        for way, sign in ((0, -1), (1, 1)):
            ref = self.view(self.at(sign * step), self.rows(step == self.count // 2, way))
            self.copy(step, way, ref, ref).wait_recv()


class Gather(Line):
    def __init__(self, *args, slot):
        super().__init__(*args)
        self.slot = slot

    def start(self, step):
        for way, sign in ((0, 1), (1, -1)):
            rows = self.rows(step == 1, way)
            src = self.view(self.at(sign * (self.count // 2 + 1 - step)), rows)
            copy = self.copy(step, way, src, self.slot(way, step - 1, rows))
            copy.start()
            self.sent.append(copy)

    def add(self, step):
        for way, sign in ((0, 1), (1, -1)):
            rows = self.rows(step == 1, way)
            here = self.view(self.at(sign * (self.count // 2 - step)), rows)
            came = self.slot(way, step - 1, rows)
            self.copy(step, way, came, came).wait_recv()
            here[...] = (here[...].astype(jnp.float32) + came[...].astype(jnp.float32)).astype(
                here.dtype
            )


def counter():
    state = [0]

    def take(count):
        base = state[0]
        state[0] += count
        return base

    return take


def block_kernel(
    cut, experts, class_ref, live_ref, x_ref, g_ref, up_ref, down_ref, mixed_ref, gup_ref, gdown_ref,
    xs, gs, part, ra2, ra1, rb2, rb1, slope_of, hid, igr, out_to, in_from, wide,
    own_sem, dsend, drecv, xsend, xrecv, gsend, grecv, rsend, rrecv,
):
    me = lax.axis_index("dp")
    e = lax.axis_index("expert")
    y, x = lax.div(me, NX), lax.rem(me, NX)
    width = x_ref.shape[1]
    lo, hi = pl.ds(0, cut), pl.ds(cut, width - cut)

    def device(yy, xx):
        return (lax.rem(yy + NY, NY) * NX + lax.rem(xx + NX, NX), e)

    xr, xl = device(y, x + 1), device(y, x - 1)
    yr, yl = device(y + 1, x), device(y - 1, x)

    n = x_ref.shape[0]
    span = n // experts

    def other(offset):
        return lax.rem(e + offset + experts, experts)

    barrier = pltpu.get_barrier_semaphore()
    for peer in [xr, xl, yr, yl] + [(me, other(d)) for d in range(1, experts)]:
        pl.semaphore_signal(barrier, inc=1, device_id=peer, device_id_type=MESH)

    def exchange(k, d, way):
        there = other(d * way)
        return pltpu.make_async_remote_copy(
            src_ref=out_to.at[k, there],
            dst_ref=in_from.at[k, e if way == 1 else there],
            send_sem=dsend.at[k, d],
            recv_sem=drecv.at[k, d],
            device_id=(me, there),
            device_id_type=MESH,
        )

    def own(k):
        return pltpu.make_async_copy(out_to.at[k, e], in_from.at[k, e], own_sem.at[k])

    near = [d for h in range(1, experts // 2 + 1) for d in sorted({h, experts - h})]

    def fill(k, table, rows):
        spread = jnp.dot(table, rows, preferred_element_type=jnp.float32)
        out_to[k] = spread.reshape(experts, PAD, width)[:, :span, :].astype(jnp.bfloat16)

    def leave(k):
        own(k).start()
        for d in near:
            copy = exchange(k, d, 1)
            copy.start()
            sent.append(copy)

    def arrive(k, table):
        own(k).wait()
        for d in near:
            exchange(k, d, -1).wait_recv()
        wide[:, :span, :] = in_from[k].astype(jnp.float32)
        flat = wide[...].reshape(experts * PAD, width).astype(jnp.bfloat16)
        return lax.dot_general(
            table, flat, (((0,), (0,)), ((), ())), preferred_element_type=jnp.float32
        ).astype(jnp.bfloat16)

    wide[...] = jnp.zeros_like(wide)
    slot = lax.broadcasted_iota(jnp.int32, (experts * PAD, n), 0)
    row = lax.broadcasted_iota(jnp.int32, (experts * PAD, n), 1)
    dense = (slot == lax.div(row, span) * PAD + lax.rem(row, span)).astype(jnp.bfloat16)
    sent = []
    table = slot_table(class_ref[...], live_ref[...], experts)
    fill(0, table, x_ref[...])
    pl.semaphore_wait(barrier, 3 + experts)
    leave(0)
    fill(1, table, g_ref[...])
    leave(1)
    xs[y, x] = arrive(0, dense)

    offsets = (0, 1, -1, 2, -2, 3, -3, 4)

    def row_of(offset):
        return lax.rem(y + offset + NY, NY)

    across = (0, 1, -1, 2)

    def column_of(offset):
        return lax.rem(x + offset + NX, NX)

    def gather_rounds(t, send_sem, recv_sem, ready):
        take, sems = counter(), (send_sem, recv_sem)
        a1 = Spread(NX, x, lambda i, r: t.at[y, i, r, lo], xr, xl, sems, take, sent)
        a2 = {
            o: Spread(
                NY, y, (lambda xx: lambda i, r: t.at[i, xx, r, lo])(column_of(o)),
                yr, yl, sems, take, sent,
            )
            for o in across
        }
        b1 = Spread(NY, y, lambda i, r: t.at[i, x, r, hi], yr, yl, sems, take, sent)
        b2 = {
            o: Spread(
                NX, x, (lambda yy: lambda i, r: t.at[yy, i, r, hi])(row_of(o)),
                xr, xl, sems, take, sent,
            )
            for o in offsets
        }

        def turn(*offs):
            for o in offs:
                b2[o].wait(1)
                b2[o].start(2)

        def relay(step, *offs):
            for o in offs:
                a2[o].wait(step)
                a2[o].start(step + 1)

        def whole(*offs):
            for o in offs:
                b2[o].wait(2)
                ready(o)

        a1.start(1)
        b1.start(1)
        a2[0].start(1)
        b2[0].start(1)
        yield
        b1.wait(1)
        b1.start(2)
        a1.wait(1)
        a1.start(2)
        for o in (1, -1):
            a2[o].start(1)
            b2[o].start(1)
        yield
        b1.wait(2)
        b1.start(3)
        b2[2].start(1)
        b2[-2].start(1)
        relay(1, 0)
        a1.wait(2)
        a2[2].start(1)
        turn(0)
        yield
        b1.wait(3)
        b1.start(4)
        b2[3].start(1)
        b2[-3].start(1)
        relay(1, 1, -1)
        turn(1, -1)
        yield
        b1.wait(4)
        b2[4].start(1)
        relay(2, 0)
        relay(1, 2)
        turn(2, -2)
        yield
        relay(2, 1, -1)
        turn(3, -3)
        relay(3, 0)
        relay(2, 2)
        whole(0)
        yield
        relay(3, 1, -1)
        turn(4)
        relay(3, 2)
        whole(1, -1)
        yield
        whole(2, -2)
        yield
        whole(3, -3)
        yield
        for o in across:
            a2[o].wait(4)
        whole(4)

    def sum_rounds():
        take, sems = counter(), (rsend, rrecv)
        a2 = {
            o: Gather(
                NY, y, (lambda xx: lambda i, r: part.at[i, xx, r, lo])(column_of(o)),
                yr, yl, sems, take, sent,
                slot=(lambda m: lambda w, s, r: ra2.at[m, w, s, r, :])(m),
            )
            for m, o in enumerate(across)
        }
        a1 = Gather(
            NX, x, lambda i, r: part.at[y, i, r, lo], xr, xl, sems, take, sent,
            slot=lambda w, s, r: ra1.at[w, s, r, :],
        )
        b1 = Gather(
            NY, y, lambda i, r: part.at[i, x, r, hi], yr, yl, sems, take, sent,
            slot=lambda w, s, r: rb1.at[w, s, r, :],
        )
        b2 = {
            o: Gather(
                NX, x, (lambda yy: lambda i, r: part.at[yy, i, r, hi])(row_of(o)),
                xr, xl, sems, take, sent,
                slot=(lambda m: lambda w, s, r: rb2.at[m, w, s, r, :])(m),
            )
            for m, o in enumerate(offsets)
        }

        def turn(*offs):
            for o in offs:
                b2[o].add(1)
                b2[o].start(2)

        def relay(step, *offs):
            for o in offs:
                a2[o].add(step)
                a2[o].start(step + 1)

        def done(*offs):
            for o in offs:
                b2[o].add(2)

        b2[4].start(1)
        a2[2].start(1)
        for o in (1, -1):
            a2[o].start(1)
            b2[3 * o].start(1)
        a2[0].start(1)
        b2[2].start(1)
        b2[-2].start(1)
        yield
        turn(4)
        relay(1, 2)
        turn(3, -3)
        relay(1, 1, -1, 0)
        for o in (1, -1, 0):
            b2[o].start(1)
        yield
        done(4)
        b1.start(1)
        relay(2, 2)
        turn(2, -2)
        relay(2, 1, -1)
        yield
        done(3, -3)
        b1.add(1)
        b1.start(2)
        relay(2, 0)
        relay(3, 2)
        turn(1, -1, 0)
        yield
        relay(3, 1, -1)
        done(2, -2)
        b1.add(2)
        b1.start(3)
        relay(3, 0)
        a2[2].add(4)
        a1.start(1)
        yield
        done(1, -1)
        b1.add(3)
        b1.start(4)
        a2[1].add(4)
        a2[-1].add(4)
        a1.add(1)
        a1.start(2)
        yield
        a2[0].add(4)
        done(0)
        b1.add(4)
        a1.add(2)

    nt = (((1,), (1,)), ((), ()))
    tn = (((0,), (0,)), ((), ()))
    chunk = NX * 32

    def forward(offset):
        c = row_of(offset)
        rows = xs[c].reshape(chunk, width)
        v = lax.dot_general(up_ref[...], rows, nt, preferred_element_type=jnp.float32)
        t = jnp.tanh(ROOT * (v + CUBE * v * v * v))
        columns = pl.ds(pl.multiple_of(c * chunk, chunk), chunk)
        slope_of[:, columns] = 0.5 * (1.0 + t) + 0.5 * v * (1.0 - t * t) * (
            ROOT * (1.0 + 3.0 * CUBE * v * v)
        )
        h = (0.5 * v * (1.0 + t)).astype(jnp.bfloat16)
        hid[:, columns] = h
        p = lax.dot_general(h, down_ref[...], tn, preferred_element_type=jnp.float32)
        part[c] = p.astype(jnp.bfloat16).reshape(NX, 32, width)

    def backward(offset):
        c = row_of(offset)
        rows = gs[c].reshape(chunk, width)
        v = lax.dot_general(down_ref[...], rows, nt, preferred_element_type=jnp.float32)
        columns = pl.ds(pl.multiple_of(c * chunk, chunk), chunk)
        igr[:, columns] = (v * slope_of[:, columns]).astype(jnp.bfloat16)

    def weight_sums(left, t, out):
        tile = min(256, width)

        def body(j, carry):
            columns = pl.ds(pl.multiple_of(j * tile, tile), tile)
            rows = t[:, :, :, columns].reshape(NY * chunk, tile)
            out[:, columns] = jnp.dot(left[...], rows, preferred_element_type=jnp.float32)
            return carry

        lax.fori_loop(0, width // tile, body, 0)

    xg = gather_rounds(xs, xsend, xrecv, forward)
    gg = gather_rounds(gs, gsend, grecv, backward)
    rg = sum_rounds()
    for _ in range(3):
        next(xg)
    gs[y, x] = arrive(1, dense)
    for _ in range(2):
        next(xg)
    for _ in range(4):
        next(gg)
        next(xg)
    next(gg)
    next(xg, None)
    for _ in range(5):
        next(rg)
        next(gg, None)
    for _ in rg:
        pass
    fill(2, dense, part[y, x])
    leave(2)
    weight_sums(hid, gs, gdown_ref)
    weight_sums(igr, xs, gup_ref)
    mixed_ref[...] = arrive(2, table)
    for copy in sent:
        copy.wait_send()


def block(labels, live, rows, grads, up, down, experts):
    n, width = rows.shape
    units = up.shape[0]
    cut = max(1, (width // 128) * 5 // 12) * 128
    rest = width - cut
    bf, f32 = jnp.bfloat16, jnp.float32
    vmem = pl.BlockSpec(memory_space=pltpu.VMEM)
    dma = lambda k: pltpu.SemaphoreType.DMA((k,))
    return pl.pallas_call(
        functools.partial(block_kernel, cut, experts),
        out_shape=(
            jax.ShapeDtypeStruct((n, width), bf),
            jax.ShapeDtypeStruct((units, width), f32),
            jax.ShapeDtypeStruct((units, width), f32),
        ),
        in_specs=[vmem] * 6,
        out_specs=(vmem,) * 3,
        scratch_shapes=[
            pltpu.VMEM((NY, NX, n, width), bf),
            pltpu.VMEM((NY, NX, n, width), bf),
            pltpu.VMEM((NY, NX, n, width), bf),
            pltpu.VMEM((NX, 2, 4, n, cut), bf),
            pltpu.VMEM((2, 2, n, cut), bf),
            pltpu.VMEM((8, 2, 2, n, rest), bf),
            pltpu.VMEM((2, 4, n, rest), bf),
            pltpu.VMEM((units, NY * NX * n), f32),
            pltpu.VMEM((units, NY * NX * n), bf),
            pltpu.VMEM((units, NY * NX * n), bf),
            pltpu.VMEM((3, experts, n // experts, width), bf),
            pltpu.VMEM((3, experts, n // experts, width), bf),
            pltpu.VMEM((experts, PAD, width), f32),
            dma(3),
            pltpu.SemaphoreType.DMA((3, experts)),
            pltpu.SemaphoreType.DMA((3, experts)),
        ]
        + [dma(SEMS)] * 6,
        compiler_params=pltpu.CompilerParams(
            collective_id=0, has_side_effects=True, vmem_limit_bytes=58 * 1024 * 1024
        ),
    )(labels, live, rows, grads, up, down)


def local(features, classes, live_counts, cotangent, up_weight, down_weight):
    expert_count = lax.axis_size("expert")
    mixed, grad_up, grad_down = block(
        classes[None, :], live_counts[None, :], features, cotangent,
        up_weight[0], down_weight[0], expert_count,
    )
    return (mixed, grad_up[None], grad_down[None])


def solution(mesh):
    placed = (
        P(("dp", "expert"), None),
        P(("dp", "expert")),
        P(("dp", "expert")),
        P(("dp", "expert"), None),
        P("expert", "dp", None),
        P("expert", "dp", None),
    )
    return jax.shard_map(
        local,
        mesh=mesh,
        in_specs=placed,
        out_specs=(P(("dp", "expert"), None), P("expert", "dp", None), P("expert", "dp", None)),
        check_vma=False,
    )
```

```python
import functools

import jax
import jax.numpy as jnp
from jax import lax
from jax.experimental import pallas as pl
from jax.experimental.pallas import tpu as pltpu
from jax.sharding import PartitionSpec as P

NY, NX = 8, 4
MESH = pl.DeviceIdType.MESH
SEMS = 76
PAD = 8
ROOT = 0.7978845608028654
CUBE = 0.044715


def slot_table(labels, live, experts):
    count = labels.shape[1]
    across = jnp.broadcast_to(labels, (count, count)).astype(jnp.float32)
    down = across.T
    sooner = lax.broadcasted_iota(jnp.int32, (count, count), 0)
    later = lax.broadcasted_iota(jnp.int32, (count, count), 1)
    earlier = jnp.where((across == down) & (sooner < later), 1.0, 0.0)
    place = jnp.sum(earlier, axis=0, keepdims=True).astype(jnp.int32)
    position = lax.broadcasted_iota(jnp.int32, (1, count), 1)
    target = jnp.where(position < live, labels * PAD + place, -1)
    slots = lax.broadcasted_iota(jnp.int32, (experts * PAD, count), 0)
    return jnp.where(slots == target, 1.0, 0.0).astype(jnp.bfloat16)


class Line:
    def __init__(self, count, here, view, right, left, sems, take, sent):
        self.count, self.here, self.view = count, here, view
        self.right, self.left = right, left
        self.send_sem, self.recv_sem = sems
        self.base = take(count)
        self.sent = sent

    def at(self, offset):
        return lax.rem(self.here + offset + self.count, self.count)

    def rows(self, half, way):
        rows = 32
        if not half:
            return pl.ds(0, rows)
        return pl.ds(0, rows // 2) if way == 0 else pl.ds(rows // 2, rows // 2)

    def copy(self, step, way, src, dst):
        k = self.base + 2 * (step - 1) + way
        return pltpu.make_async_remote_copy(
            src_ref=src,
            dst_ref=dst,
            send_sem=self.send_sem.at[k],
            recv_sem=self.recv_sem.at[k],
            device_id=self.right if way == 0 else self.left,
            device_id_type=MESH,
        )


class Spread(Line):
    def start(self, step):
        for way, sign in ((0, -1), (1, 1)):
            ref = self.view(self.at(sign * (step - 1)), self.rows(step == self.count // 2, way))
            copy = self.copy(step, way, ref, ref)
            copy.start()
            self.sent.append(copy)

    def wait(self, step):
        for way, sign in ((0, -1), (1, 1)):
            ref = self.view(self.at(sign * step), self.rows(step == self.count // 2, way))
            self.copy(step, way, ref, ref).wait_recv()


class Gather(Line):
    def __init__(self, *args, slot):
        super().__init__(*args)
        self.slot = slot

    def start(self, step):
        for way, sign in ((0, 1), (1, -1)):
            rows = self.rows(step == 1, way)
            src = self.view(self.at(sign * (self.count // 2 + 1 - step)), rows)
            copy = self.copy(step, way, src, self.slot(way, step - 1, rows))
            copy.start()
            self.sent.append(copy)

    def add(self, step):
        for way, sign in ((0, 1), (1, -1)):
            rows = self.rows(step == 1, way)
            here = self.view(self.at(sign * (self.count // 2 - step)), rows)
            came = self.slot(way, step - 1, rows)
            self.copy(step, way, came, came).wait_recv()
            here[...] = (here[...].astype(jnp.float32) + came[...].astype(jnp.float32)).astype(
                here.dtype
            )


def counter():
    state = [0]

    def take(count):
        base = state[0]
        state[0] += count
        return base

    return take


def block_kernel(
    cut, experts, class_ref, live_ref, x_ref, g_ref, up_ref, down_ref, mixed_ref, gup_ref, gdown_ref,
    xs, gs, part, ra2, ra1, rb2, rb1, slope_of, hid, igr, out_to, in_from, wide,
    own_sem, dsend, drecv, xsend, xrecv, gsend, grecv, rsend, rrecv,
):
    me = lax.axis_index("dp")
    e = lax.axis_index("expert")
    y, x = lax.div(me, NX), lax.rem(me, NX)
    width = x_ref.shape[1]
    lo, hi = pl.ds(0, cut), pl.ds(cut, width - cut)

    def device(yy, xx):
        return (lax.rem(yy + NY, NY) * NX + lax.rem(xx + NX, NX), e)

    xr, xl = device(y, x + 1), device(y, x - 1)
    yr, yl = device(y + 1, x), device(y - 1, x)

    n = x_ref.shape[0]
    span = n // experts

    def other(offset):
        return lax.rem(e + offset + experts, experts)

    barrier = pltpu.get_barrier_semaphore()
    for peer in [xr, xl, yr, yl] + [(me, other(d)) for d in range(1, experts)]:
        pl.semaphore_signal(barrier, inc=1, device_id=peer, device_id_type=MESH)

    def exchange(k, d, way):
        there = other(d * way)
        return pltpu.make_async_remote_copy(
            src_ref=out_to.at[k, there],
            dst_ref=in_from.at[k, e if way == 1 else there],
            send_sem=dsend.at[k, d],
            recv_sem=drecv.at[k, d],
            device_id=(me, there),
            device_id_type=MESH,
        )

    def own(k):
        return pltpu.make_async_copy(out_to.at[k, e], in_from.at[k, e], own_sem.at[k])

    far_first = [d for h in range(experts // 2, 0, -1) for d in sorted({h, experts - h})]

    def fill(k, table, rows):
        spread = jnp.dot(table, rows, preferred_element_type=jnp.float32)
        out_to[k] = spread.reshape(experts, PAD, width)[:, :span, :].astype(jnp.bfloat16)

    def leave(k):
        own(k).start()
        for d in far_first:
            copy = exchange(k, d, 1)
            copy.start()
            sent.append(copy)

    def arrive(k, table):
        own(k).wait()
        for d in far_first:
            exchange(k, d, -1).wait_recv()
        wide[:, :span, :] = in_from[k].astype(jnp.float32)
        flat = wide[...].reshape(experts * PAD, width).astype(jnp.bfloat16)
        return lax.dot_general(
            table, flat, (((0,), (0,)), ((), ())), preferred_element_type=jnp.float32
        ).astype(jnp.bfloat16)

    wide[...] = jnp.zeros_like(wide)
    slot = lax.broadcasted_iota(jnp.int32, (experts * PAD, n), 0)
    row = lax.broadcasted_iota(jnp.int32, (experts * PAD, n), 1)
    dense = (slot == lax.div(row, span) * PAD + lax.rem(row, span)).astype(jnp.bfloat16)
    sent = []
    table = slot_table(class_ref[...], live_ref[...], experts)
    fill(0, table, x_ref[...])
    pl.semaphore_wait(barrier, 3 + experts)
    leave(0)
    xs[y, x] = arrive(0, dense)

    offsets = (0, 1, -1, 2, -2, 3, -3, 4)

    def row_of(offset):
        return lax.rem(y + offset + NY, NY)

    across = (0, 1, -1, 2)

    def column_of(offset):
        return lax.rem(x + offset + NX, NX)

    def gather_rounds(t, send_sem, recv_sem, ready):
        take, sems = counter(), (send_sem, recv_sem)
        a1 = Spread(NX, x, lambda i, r: t.at[y, i, r, lo], xr, xl, sems, take, sent)
        a2 = {
            o: Spread(
                NY, y, (lambda xx: lambda i, r: t.at[i, xx, r, lo])(column_of(o)),
                yr, yl, sems, take, sent,
            )
            for o in across
        }
        b1 = Spread(NY, y, lambda i, r: t.at[i, x, r, hi], yr, yl, sems, take, sent)
        b2 = {
            o: Spread(
                NX, x, (lambda yy: lambda i, r: t.at[yy, i, r, hi])(row_of(o)),
                xr, xl, sems, take, sent,
            )
            for o in offsets
        }

        def turn(*offs):
            for o in offs:
                b2[o].wait(1)
                b2[o].start(2)

        def relay(step, *offs):
            for o in offs:
                a2[o].wait(step)
                a2[o].start(step + 1)

        def whole(*offs):
            for o in offs:
                b2[o].wait(2)
                ready(o)

        a1.start(1)
        b1.start(1)
        a2[0].start(1)
        b2[0].start(1)
        yield
        b1.wait(1)
        b1.start(2)
        a1.wait(1)
        a1.start(2)
        for o in (1, -1):
            a2[o].start(1)
            b2[o].start(1)
        yield
        b1.wait(2)
        b1.start(3)
        b2[2].start(1)
        b2[-2].start(1)
        relay(1, 0)
        a1.wait(2)
        a2[2].start(1)
        turn(0)
        yield
        b1.wait(3)
        b1.start(4)
        b2[3].start(1)
        b2[-3].start(1)
        relay(1, 1, -1)
        turn(1, -1)
        yield
        b1.wait(4)
        b2[4].start(1)
        relay(2, 0)
        relay(1, 2)
        turn(2, -2)
        yield
        relay(2, 1, -1)
        turn(3, -3)
        relay(3, 0)
        relay(2, 2)
        whole(0)
        yield
        relay(3, 1, -1)
        turn(4)
        relay(3, 2)
        whole(1, -1)
        yield
        whole(2, -2)
        yield
        whole(3, -3)
        yield
        for o in across:
            a2[o].wait(4)
        whole(4)

    def sum_rounds():
        take, sems = counter(), (rsend, rrecv)
        a2 = {
            o: Gather(
                NY, y, (lambda xx: lambda i, r: part.at[i, xx, r, lo])(column_of(o)),
                yr, yl, sems, take, sent,
                slot=(lambda m: lambda w, s, r: ra2.at[m, w, s, r, :])(m),
            )
            for m, o in enumerate(across)
        }
        a1 = Gather(
            NX, x, lambda i, r: part.at[y, i, r, lo], xr, xl, sems, take, sent,
            slot=lambda w, s, r: ra1.at[w, s, r, :],
        )
        b1 = Gather(
            NY, y, lambda i, r: part.at[i, x, r, hi], yr, yl, sems, take, sent,
            slot=lambda w, s, r: rb1.at[w, s, r, :],
        )
        b2 = {
            o: Gather(
                NX, x, (lambda yy: lambda i, r: part.at[yy, i, r, hi])(row_of(o)),
                xr, xl, sems, take, sent,
                slot=(lambda m: lambda w, s, r: rb2.at[m, w, s, r, :])(m),
            )
            for m, o in enumerate(offsets)
        }

        def turn(*offs):
            for o in offs:
                b2[o].add(1)
                b2[o].start(2)

        def relay(step, *offs):
            for o in offs:
                a2[o].add(step)
                a2[o].start(step + 1)

        def done(*offs):
            for o in offs:
                b2[o].add(2)

        b2[4].start(1)
        a2[2].start(1)
        for o in (1, -1):
            a2[o].start(1)
            b2[3 * o].start(1)
        a2[0].start(1)
        b2[2].start(1)
        b2[-2].start(1)
        yield
        turn(4)
        relay(1, 2)
        turn(3, -3)
        relay(1, 1, -1, 0)
        for o in (1, -1, 0):
            b2[o].start(1)
        yield
        done(4)
        b1.start(1)
        relay(2, 2)
        turn(2, -2)
        relay(2, 1, -1)
        yield
        done(3, -3)
        b1.add(1)
        b1.start(2)
        relay(2, 0)
        relay(3, 2)
        turn(1, -1, 0)
        yield
        relay(3, 1, -1)
        done(2, -2)
        b1.add(2)
        b1.start(3)
        relay(3, 0)
        a2[2].add(4)
        a1.start(1)
        yield
        done(1, -1)
        b1.add(3)
        b1.start(4)
        a2[1].add(4)
        a2[-1].add(4)
        a1.add(1)
        a1.start(2)
        yield
        a2[0].add(4)
        done(0)
        b1.add(4)
        a1.add(2)

    nt = (((1,), (1,)), ((), ()))
    tn = (((0,), (0,)), ((), ()))
    chunk = NX * 32

    def forward(offset):
        c = row_of(offset)
        rows = xs[c].reshape(chunk, width)
        v = lax.dot_general(up_ref[...], rows, nt, preferred_element_type=jnp.float32)
        t = jnp.tanh(ROOT * (v + CUBE * v * v * v))
        columns = pl.ds(pl.multiple_of(c * chunk, chunk), chunk)
        slope_of[:, columns] = 0.5 * (1.0 + t) + 0.5 * v * (1.0 - t * t) * (
            ROOT * (1.0 + 3.0 * CUBE * v * v)
        )
        h = (0.5 * v * (1.0 + t)).astype(jnp.bfloat16)
        hid[:, columns] = h
        p = lax.dot_general(h, down_ref[...], tn, preferred_element_type=jnp.float32)
        part[c] = p.astype(jnp.bfloat16).reshape(NX, 32, width)

    def backward(offset):
        c = row_of(offset)
        rows = gs[c].reshape(chunk, width)
        v = lax.dot_general(down_ref[...], rows, nt, preferred_element_type=jnp.float32)
        columns = pl.ds(pl.multiple_of(c * chunk, chunk), chunk)
        igr[:, columns] = (v * slope_of[:, columns]).astype(jnp.bfloat16)

    def weight_sums(left, t, out):
        tile = min(256, width)

        def body(j, carry):
            columns = pl.ds(pl.multiple_of(j * tile, tile), tile)
            rows = t[:, :, :, columns].reshape(NY * chunk, tile)
            out[:, columns] = jnp.dot(left[...], rows, preferred_element_type=jnp.float32)
            return carry

        lax.fori_loop(0, width // tile, body, 0)

    xg = gather_rounds(xs, xsend, xrecv, forward)
    gg = gather_rounds(gs, gsend, grecv, backward)
    rg = sum_rounds()
    next(xg)
    fill(1, table, g_ref[...])
    leave(1)
    for _ in range(4):
        next(xg)
    gs[y, x] = arrive(1, dense)
    for _ in range(4):
        next(gg)
        next(xg)
    next(gg)
    next(xg, None)
    for _ in range(5):
        next(rg)
        next(gg, None)
    for _ in rg:
        pass
    fill(2, dense, part[y, x])
    leave(2)
    weight_sums(hid, gs, gdown_ref)
    weight_sums(igr, xs, gup_ref)
    mixed_ref[...] = arrive(2, table)
    for copy in sent:
        copy.wait_send()


def block(labels, live, rows, grads, up, down, experts):
    n, width = rows.shape
    units = up.shape[0]
    cut = max(1, (width // 128) * 5 // 12) * 128
    rest = width - cut
    bf, f32 = jnp.bfloat16, jnp.float32
    vmem = pl.BlockSpec(memory_space=pltpu.VMEM)
    dma = lambda k: pltpu.SemaphoreType.DMA((k,))
    return pl.pallas_call(
        functools.partial(block_kernel, cut, experts),
        out_shape=(
            jax.ShapeDtypeStruct((n, width), bf),
            jax.ShapeDtypeStruct((units, width), f32),
            jax.ShapeDtypeStruct((units, width), f32),
        ),
        in_specs=[vmem] * 6,
        out_specs=(vmem,) * 3,
        scratch_shapes=[
            pltpu.VMEM((NY, NX, n, width), bf),
            pltpu.VMEM((NY, NX, n, width), bf),
            pltpu.VMEM((NY, NX, n, width), bf),
            pltpu.VMEM((NX, 2, 4, n, cut), bf),
            pltpu.VMEM((2, 2, n, cut), bf),
            pltpu.VMEM((8, 2, 2, n, rest), bf),
            pltpu.VMEM((2, 4, n, rest), bf),
            pltpu.VMEM((units, NY * NX * n), f32),
            pltpu.VMEM((units, NY * NX * n), bf),
            pltpu.VMEM((units, NY * NX * n), bf),
            pltpu.VMEM((3, experts, n // experts, width), bf),
            pltpu.VMEM((3, experts, n // experts, width), bf),
            pltpu.VMEM((experts, PAD, width), f32),
            dma(3),
            pltpu.SemaphoreType.DMA((3, experts)),
            pltpu.SemaphoreType.DMA((3, experts)),
        ]
        + [dma(SEMS)] * 6,
        compiler_params=pltpu.CompilerParams(
            collective_id=0, has_side_effects=True, vmem_limit_bytes=58 * 1024 * 1024
        ),
    )(labels, live, rows, grads, up, down)


def local(features, classes, live_counts, cotangent, up_weight, down_weight):
    expert_count = lax.axis_size("expert")
    mixed, grad_up, grad_down = block(
        classes[None, :], live_counts[None, :], features, cotangent,
        up_weight[0], down_weight[0], expert_count,
    )
    return (mixed, grad_up[None], grad_down[None])


def solution(mesh):
    placed = (
        P(("dp", "expert"), None),
        P(("dp", "expert")),
        P(("dp", "expert")),
        P(("dp", "expert"), None),
        P("expert", "dp", None),
        P("expert", "dp", None),
    )
    return jax.shard_map(
        local,
        mesh=mesh,
        in_specs=placed,
        out_specs=(P(("dp", "expert"), None), P("expert", "dp", None), P("expert", "dp", None)),
        check_vma=False,
    )
```
